32 devices in a mesh: batch: 4 (over z), row: 2 (over y), col: 4 (over x, core).
Axes of the slice: x: 2, y: 2, z: 4, core: 2. Of those that a mesh axis runs over, the one named last changes fastest.
Arguments:
- tokens: bfloat16 [16384, 1280], P(('batch', 'row'), 'col'), may hold values from -6 to 6
- prefix: int32 [16], P(('batch', 'col')), may hold values from 102 to 512
- gain_attn: float32 [1280], P('col'), may hold values from 0.5 to 1.5
- w_qkv: bfloat16 [1280, 16, 240], P('col', 'row'), may hold values from -0.15625 to 0.15625
- query_scale: float32 [80], replicated, may hold values from -1 to 1
- w_out: bfloat16 [1280, 1280], P('row', 'col'), may hold values from -1.25 to 1.25
- gain_mlp: float32 [1280], P('col'), may hold values from 0.5 to 1.5
- w_up: bfloat16 [1280, 1280], P('col', 'row'), may hold values from -0.15625 to 0.15625
- b_up: float32 [1280], P('row'), may hold values from -3 to 3
- w_down: bfloat16 [1280, 1280], P('row', 'col'), may hold values from -0.15625 to 0.15625
- b_down: float32 [1280], P('col'), may hold values from -3 to 3
- cotangent: bfloat16 [16384, 1280], P(('batch', 'row'), 'col'), may hold values from -6 to 6
Outputs:
- output: bfloat16 [16384, 1280], P(('batch', 'row'), 'col')
- d_tokens: float32 [16384, 1280], P(('batch', 'row'), 'col')
- d_gain_attn: float32 [1280], P('col')
- d_w_qkv: float32 [1280, 16, 240], P('col', 'row')
- d_query_scale: float32 [80], replicated
- d_w_out: float32 [1280, 1280], P('row', 'col')
- d_gain_mlp: float32 [1280], P('col')
- d_w_up: float32 [1280, 1280], P('col', 'row')
- d_b_up: float32 [1280], P('row')
- d_w_down: float32 [1280, 1280], P('row', 'col')
- d_b_down: float32 [1280], P('col')
The draws below stay inside these ranges and needn't reach their ends.
Inputs may be any that keep to these rules, and one draw needn't show every extreme that they name: Each sequence's prefix holds between a tenth and a half of its 1024 tokens.
All inputs are finite; a program needn't handle non-finite values.
Results may differ from the reference program's by a relative error of at most 0.012.
The reference program's roundings to bfloat16 on the way count: a program that leaves them out, or rounds other values in their place, can miss the bound.
Values may be sent and summed in bfloat16 or wider, within the bound.
No kernel may reach another device: no remote copies, remote signals or barrier semaphores. Data moves between devices by JAX's collectives and lax.ppermute only.
A program may use at most 320 MiB of HBM per device.

```python
import math
import jax
import jax.numpy as jnp
from jax import lax

D = 1280
FF = 1280
HEADS = 16
HD = 80
LENGTH = 1024
SEQS = 16
TOKENS = 16384


def set_ends(values, rng, low, top_value):
    longest = values.shape.index(max(values.shape))
    spots = []
    for shift in (0, 1):
        where = [jax.random.randint(jax.random.fold_in(rng, axis), (), 0, length) for axis, length in enumerate(values.shape)]
        where[longest] = (where[longest] + shift) % values.shape[longest]
        spots.append(tuple(where))
    return values.at[spots[0]].set(low).at[spots[1]].set(top_value)


def levels(key, extent, cuts, least, largest):
    def one(axis_at, shards_of):
        heights = jax.random.uniform(jax.random.fold_in(jax.random.fold_in(key, 6), axis_at), (shards_of,), jnp.float32, least / len(cuts), largest / len(cuts))
        return jnp.repeat(jnp.exp(heights), extent[axis_at] // shards_of).reshape((-1,) + (1,) * (len(extent) - axis_at - 1))

    gain = one(*cuts[0])
    for cut in cuts[1:]:
        gain = gain * one(*cut)
    return gain


def bell_draw(key, extent, scale, bound, split=(), kind=jnp.bfloat16):
    factor_of = levels(key, extent, split, -0.22, 0.18) if split else 1.0
    array = jax.random.normal(key, extent, jnp.float32) * scale * factor_of
    return jnp.minimum(jnp.maximum(array, -bound), bound).astype(kind)


def setup_inputs(seed: int = 0) -> dict:
    seeds = jax.random.split(jax.random.key(seed), 13)
    tokens = bell_draw(seeds[0], (TOKENS, D), 1.0, 6.0, ((0, 8), (1, 4)))
    prefix = set_ends(jax.random.randint(seeds[1], (SEQS,), LENGTH // 10, LENGTH // 2 + 1), jax.random.fold_in(seeds[1], 1), LENGTH // 10, (LENGTH // 2 + 1) - 1).astype(jnp.int32)
    gain_attn = jnp.clip(1.0 + 0.1 * jax.random.normal(seeds[2], (D,), jnp.float32), 0.5, 1.5)
    w_qkv = bell_draw(seeds[3], (D, HEADS, 3 * HD), D ** -0.5, 0.15625, ((0, 4), (1, 2)))
    query_scale = jnp.clip(jax.random.uniform(seeds[4], (HD,), jnp.float32, -1.0, 1.0), -1.0, 1.0)
    w_out = bell_draw(seeds[5], (D, D), (D // 64) ** -0.5, 1.25, ((0, 2), (1, 4)))
    gain_mlp = jnp.clip(1.0 + 0.1 * jax.random.normal(seeds[6], (D,), jnp.float32), 0.5, 1.5)
    w_up = bell_draw(seeds[7], (D, FF), D ** -0.5, 0.15625, ((0, 4), (1, 2)))
    b_up = bell_draw(seeds[8], (FF,), 0.5, 3.0, ((0, 2),), jnp.float32)
    w_down = bell_draw(seeds[9], (FF, D), FF ** -0.5, 0.15625, ((0, 2), (1, 4)))
    b_down = bell_draw(seeds[10], (D,), 0.5, 3.0, ((0, 4),), jnp.float32)
    cotangent = bell_draw(seeds[11], (TOKENS, D), 1.0, 6.0, ((0, 8), (1, 4)))
    return {"tokens": tokens, "prefix": prefix, "gain_attn": gain_attn, "w_qkv": w_qkv, "query_scale": query_scale, "w_out": w_out, "gain_mlp": gain_mlp, "w_up": w_up, "b_up": b_up, "w_down": w_down, "b_down": b_down, "cotangent": cotangent}


QK_BASE = 1.442695041
EPS = 1e-06
MASKED = -1e+30
HIGHEST = lax.Precision.HIGHEST

@jax.custom_vjp
def low(v):
    return lax.optimization_barrier(v.astype(jnp.bfloat16)).astype(jnp.float32)

@jax.custom_vjp
def low_back(v):
    return v

def low_keep(v):
    return (low(v), None)

def low_pass(kept, grad):
    return (grad,)

def back_keep(v):
    return (v, None)

def back_low(kept, grad):
    return (low(grad),)
low.defvjp(low_keep, low_pass)
low_back.defvjp(back_keep, back_low)

def rms_norm(values, norm_gain):
    statistic = lax.optimization_barrier(jnp.mean(values * values, axis=-1, keepdims=True))
    return values * lax.rsqrt(statistic + EPS) * norm_gain

def visible_mask(prefix_len):
    position = jnp.arange(LENGTH)
    return (position[None, :] < prefix_len) | (position[None, :] <= position[:, None])

def attend_one(pieces):
    queries, key_rows, values, prefix_len = pieces
    scores = low_back(jnp.einsum('qhd,khd->hqk', queries, key_rows, precision=HIGHEST))
    scores = jnp.where(visible_mask(prefix_len)[None], scores, MASKED)
    highest = lax.optimization_barrier(jnp.max(scores, axis=-1, keepdims=True))
    unscaled = jnp.exp(scores - highest)
    attn_probs = unscaled / lax.optimization_barrier(jnp.sum(unscaled, axis=-1, keepdims=True))
    return jnp.einsum('hqk,khd->qhd', low(attn_probs), values, precision=HIGHEST)

def layer(tokens, gain_attn, w_qkv, query_scale, w_out, gain_mlp, w_up, b_up, w_down, b_down, prefix):
    seq_count = prefix.shape[0]
    normed = low(rms_norm(tokens, gain_attn))
    mixed_heads = jnp.dot(normed, w_qkv.reshape(D, HEADS * 3 * HD), precision=HIGHEST).reshape(-1, HEADS, 3, HD)
    factor = QK_BASE / math.sqrt(HD) * jax.nn.softplus(query_scale)
    queries = low(low_back(mixed_heads[:, :, 0]) * factor)
    key_rows = low_back(low(mixed_heads[:, :, 1]))
    values = low_back(low(mixed_heads[:, :, 2]))
    shape_seq = (seq_count, LENGTH, HEADS, HD)
    attended = lax.map(jax.checkpoint(attend_one), (queries.reshape(shape_seq), key_rows.reshape(shape_seq), values.reshape(shape_seq), prefix))
    attended = low_back(low(attended.reshape(-1, HEADS * HD)))
    middle = tokens + low_back(jnp.dot(attended, w_out, precision=HIGHEST))
    normed_mlp = low(rms_norm(middle, gain_mlp))
    before = low_back(jnp.dot(normed_mlp, w_up, precision=HIGHEST) + b_up)
    hidden = low(jax.nn.silu(before))
    return middle + jnp.dot(hidden, w_down, precision=HIGHEST) + b_down

def reference(tokens, prefix, gain_attn, w_qkv, query_scale, w_out, gain_mlp, w_up, b_up, w_down, b_down, cotangent):
    group_seqs = math.gcd(SEQS, 4)
    blocks = SEQS // group_seqs
    params = (gain_attn.astype(jnp.float32), w_qkv.astype(jnp.float32), query_scale.astype(jnp.float32), w_out.astype(jnp.float32), gain_mlp.astype(jnp.float32), w_up.astype(jnp.float32), b_up.astype(jnp.float32), w_down.astype(jnp.float32), b_down.astype(jnp.float32))

    def one_block(totals, block_data):
        block_rows, grads_in, lengths = block_data

        def local_layer(rows_in, params_in):
            return layer(rows_in, params_in[0], params_in[1], params_in[2], params_in[3], params_in[4], params_in[5], params_in[6], params_in[7], params_in[8], lengths)
        result, pullback = jax.vjp(local_layer, block_rows, params)
        d_rows, d_params = pullback(grads_in)
        totals = jax.tree.map(jnp.add, totals, d_params)
        return (totals, (result.astype(jnp.bfloat16), d_rows))
    zero_grads = jax.tree.map(jnp.zeros_like, params)
    stacked = (tokens.astype(jnp.float32).reshape(blocks, group_seqs * LENGTH, D), cotangent.astype(jnp.float32).reshape(blocks, group_seqs * LENGTH, D), prefix.reshape(blocks, group_seqs))
    totals, (outputs, d_tokens) = lax.scan(one_block, zero_grads, stacked)
    return (outputs.reshape(TOKENS, D), d_tokens.reshape(TOKENS, D), totals[0], totals[1], totals[2], totals[3], totals[4], totals[5], totals[6], totals[7], totals[8])
```

```python
import math

import jax
import jax.numpy as jnp
from jax import lax
from jax.experimental import pallas as pl
from jax.experimental.pallas import tpu as pltpu
from jax.sharding import PartitionSpec as P

D = 1280
FF = 1280
HD = 80


QK_BASE = 1.442695041
EPS = 1e-06
MASKED = -1e30
LOG2E = 1.4426950408889634


BF = jnp.bfloat16
F32 = jnp.float32


def dot(left, right, left_dim, right_dim, kind=F32):
    return lax.dot_general(
        left, right, (((left_dim,), (right_dim,)), ((), ())), preferred_element_type=kind
    )


def swap(values, axis, bit, size):
    return lax.ppermute(values, axis, [(i, i ^ bit) for i in range(size)])


def _tiles(length):
    return max(length // 4, 128)


def _visible(scores, key_start, query_start, prefix):
    keys = key_start + lax.broadcasted_iota(jnp.int32, scores.shape, 0)
    queries = query_start + lax.broadcasted_iota(jnp.int32, scores.shape, 1)
    return jnp.where((keys < prefix) | (keys <= queries), scores, MASKED)


def _join(buffer, own_ref, other_ref, core, width):
    buffer[:, pl.ds(pl.multiple_of(core * width, 128), width)] = own_ref[...]
    buffer[:, pl.ds(pl.multiple_of((1 - core) * width, 128), width)] = other_ref[...]


def _split(buffer, own_ref, other_ref, core, width):
    own_ref[...] = buffer[:, pl.ds(pl.multiple_of(core * width, 128), width)]
    other_ref[...] = buffer[:, pl.ds(pl.multiple_of((1 - core) * width, 128), width)]


def attend_kernel(scalars, own_ref, other_ref, o_own_ref, o_other_ref, mass_ref, qkv, out):
    prefix, core = scalars[0], scalars[1]
    width = own_ref.shape[1]
    length = 2 * width
    tile = _tiles(length)
    _join(qkv, own_ref, other_ref, core, width)
    keys = qkv[HD : 2 * HD, :].T
    for start in range(0, length, tile):
        reach = max(start + tile, length // 2)
        scores = dot(keys[:reach], qkv[:HD, start : start + tile], 1, 0)
        low = 0 if start < length // 2 else start
        masked = _visible(scores[low:reach], low, start, prefix)
        scores = masked if low == 0 else jnp.concatenate([scores[:low], masked], axis=0)
        highest = jnp.max(scores, axis=0, keepdims=True) * LOG2E
        unscaled = jnp.exp2(scores * LOG2E - highest)
        total = jnp.sum(unscaled, axis=0, keepdims=True)
        probs = (unscaled * (1.0 / total)).astype(BF)
        out[:, start : start + tile] = dot(qkv[2 * HD :, :reach], probs, 1, 0).astype(BF)
        mass_ref[:, start : start + tile] = highest + jnp.log(total) * LOG2E
    _split(out, o_own_ref, o_other_ref, core, width)


def attend_back_kernel(
    scalars, factor_ref, own_ref, other_ref, o_own_ref, o_other_ref, g_own_ref, g_other_ref, mass_ref,
    d_own_ref, d_other_ref, d_factor_ref, qkv, out, grad, d_qkv, d_keys, d_values,
):
    prefix, core = scalars[0], scalars[1]
    width = own_ref.shape[1]
    length = 2 * width
    tile = _tiles(length)
    _join(qkv, own_ref, other_ref, core, width)
    _join(out, o_own_ref, o_other_ref, core, width)
    _join(grad, g_own_ref, g_other_ref, core, width)
    queries = qkv[:HD, :].T
    keys = qkv[HD : 2 * HD, :].T
    values = qkv[2 * HD :, :].T
    grads = grad[...].T
    d_keys[...] = jnp.zeros_like(d_keys)
    d_values[...] = jnp.zeros_like(d_values)
    d_factor = jnp.zeros((HD, 128), F32)
    for start in range(0, length, tile):
        reach = max(start + tile, length // 2)
        here = slice(start, start + tile)
        scores = dot(keys[:reach], qkv[:HD, here], 1, 0)
        low = 0 if start < length // 2 else start
        masked = _visible(scores[low:reach], low, start, prefix)
        scores = masked if low == 0 else jnp.concatenate([scores[:low], masked], axis=0)
        probs = jnp.exp2(scores * LOG2E - mass_ref[:, here])
        d_values[:reach] += dot(probs.astype(BF), grads[here], 1, 0)
        d_probs = dot(values[:reach], grad[:, here], 1, 0)
        centre = jnp.sum(grad[:, here].astype(F32) * out[:, here].astype(F32), axis=0, keepdims=True)
        d_scores = (probs * (d_probs - centre)).astype(BF)
        d_keys[:reach] += dot(d_scores, queries[here], 1, 0)
        d_queries = dot(qkv[HD : 2 * HD, :reach], d_scores, 1, 0)
        product = d_queries * qkv[:HD, here].astype(F32)
        for lane in range(0, tile, 128):
            d_factor = d_factor + product[:, lane : lane + 128]
        d_qkv[:HD, here] = (d_queries * factor_ref[...]).astype(BF)
    d_factor_ref[...] = d_factor
    d_qkv[HD : 2 * HD, :] = d_keys[...].T.astype(BF)
    d_qkv[2 * HD :, :] = d_values[...].T.astype(BF)
    _split(d_qkv, d_own_ref, d_other_ref, core, width)


def _head(rows, width):
    return pl.BlockSpec((rows, width), lambda h, s: (h, 0))


def attend(scalars, own, other):
    heads, width = own.shape[0] // (3 * HD), own.shape[1]
    length = 2 * width
    return pl.pallas_call(
        attend_kernel,
        grid_spec=pltpu.PrefetchScalarGridSpec(
            num_scalar_prefetch=1,
            grid=(heads,),
            in_specs=[_head(3 * HD, width)] * 2,
            out_specs=[_head(HD, width)] * 2
            + [pl.BlockSpec((None, 1, length), lambda h, s: (h, 0, 0))],
            scratch_shapes=[pltpu.VMEM((3 * HD, length), BF), pltpu.VMEM((HD, length), BF)],
        ),
        out_shape=[jax.ShapeDtypeStruct((heads * HD, width), BF)] * 2
        + [jax.ShapeDtypeStruct((heads, 1, length), F32)],
        cost_estimate=pl.CostEstimate(
            flops=4 * heads * length * length * 128,
            bytes_accessed=4 * heads * length * 4 * HD,
            transcendentals=heads * length * length,
        ),
        name="attend",
    )(scalars, own, other)


def attend_back(scalars, factor, own, other, o_own, o_other, g_own, g_other, mass):
    heads, width = own.shape[0] // (3 * HD), own.shape[1]
    length = 2 * width
    return pl.pallas_call(
        attend_back_kernel,
        grid_spec=pltpu.PrefetchScalarGridSpec(
            num_scalar_prefetch=1,
            grid=(heads,),
            in_specs=[pl.BlockSpec((HD, 1), lambda h, s: (0, 0))]
            + [_head(3 * HD, width)] * 2
            + [_head(HD, width)] * 4
            + [pl.BlockSpec((None, 1, length), lambda h, s: (h, 0, 0))],
            out_specs=[_head(3 * HD, width)] * 2 + [_head(HD, 128)],
            scratch_shapes=[
                pltpu.VMEM((3 * HD, length), BF),
                pltpu.VMEM((HD, length), BF),
                pltpu.VMEM((HD, length), BF),
                pltpu.VMEM((3 * HD, length), BF),
                pltpu.VMEM((length, HD), F32),
                pltpu.VMEM((length, HD), F32),
            ],
        ),
        out_shape=[jax.ShapeDtypeStruct((heads * 3 * HD, width), BF)] * 2
        + [jax.ShapeDtypeStruct((heads * HD, 128), F32)],
        cost_estimate=pl.CostEstimate(
            flops=10 * heads * length * length * 128,
            bytes_accessed=4 * heads * length * 10 * HD,
            transcendentals=heads * length * length,
        ),
        name="attend_back",
    )(scalars, factor, own, other, o_own, o_other, g_own, g_other, mass)


def gathered_plan(rows, cols):
    across = cols // 2

    def swap_core(v):
        return swap(v, "col", 1, cols)

    def swap_across(v):
        return swap(v, "col", 2, cols)

    def swap_row(v):
        return swap(v, "row", 1, rows)

    def take(v, index, width, axis=0):
        return lax.dynamic_slice_in_dim(v, index * width, width, axis)

    def spread(block, place):
        x, core = place
        count, width = block.shape[0] // cols, block.shape[1]
        away = swap_across(take(block, 1 - x, 2 * count))
        both = jnp.stack([take(block, x, 2 * count), away]).reshape(2, 2, count, width)
        near = lax.dynamic_index_in_dim(both, core, 1, False)
        far = swap_core(lax.dynamic_index_in_dim(both, 1 - core, 1, False))
        return jnp.concatenate([near[0], near[1], far[0], far[1]], axis=1)

    def collect(whole, place):
        x, core = place
        count, half = whole.shape[0], whole.shape[1] // 2
        far = swap_core(whole[:, half:])
        near = whole[:, :half]
        both = jnp.where(core == 0, jnp.concatenate([near, far]), jnp.concatenate([far, near]))
        away = swap_across(both[:, half // 2 :])
        here = both[:, : half // 2]
        return jnp.where(x == 0, jnp.concatenate([here, away]), jnp.concatenate([away, here]))

    def gather(piece):
        half = piece.shape[0] // 2
        first, second = piece[:half], piece[half:]
        first_x = swap_across(first)
        second_y = swap_row(second)
        first_y = swap_row(jnp.stack([first, first_x]))
        second_x = swap_across(jnp.stack([second, second_y]))
        own = [
            [
                jnp.concatenate([first, second]),
                jnp.concatenate([first_y[0], second_y]),
            ],
            [
                jnp.concatenate([first_x, second_x[0]]),
                jnp.concatenate([first_y[1], second_x[1]]),
            ],
        ]
        own = jnp.concatenate([jnp.concatenate(pair, axis=1) for pair in own])
        return jnp.concatenate([own, swap_core(own)])

    def scatter(keep, send):
        total = (keep.astype(F32) + swap_core(send).astype(F32)).astype(BF)
        block, width = total.shape[0] // 2, total.shape[1] // 2
        half = block // 2
        first = [total[:half], total[block : block + half]]
        second = [total[half:block], total[block + half :]]
        first_x = swap_across(first[1])
        second = jnp.concatenate(second)
        second_y = swap_row(second[:, width:])
        first = (first[0].astype(F32) + first_x.astype(F32)).astype(BF)
        second = (second[:, :width].astype(F32) + second_y.astype(F32)).astype(BF)
        first_y = swap_row(first[:, width:])
        second_x = swap_across(second[half:])
        return jnp.concatenate(
            [
                first[:, :width].astype(F32) + first_y.astype(F32),
                second[:half].astype(F32) + second_x.astype(F32),
            ]
        )

    def shards(
        tokens, prefix, gain_attn, w_qkv, query_scale, w_out, gain_mlp, w_up, b_up, w_down, b_down, cotangent
    ):
        col, row = lax.axis_index("col"), lax.axis_index("row")
        place = (col // 2, col % 2)
        core = place[1]
        width = gain_attn.shape[0]
        hidden_width = b_up.shape[0]
        block_cols = w_qkv.shape[1] * w_qkv.shape[2]

        small = jnp.concatenate(
            [gain_attn, gain_mlp, b_down, prefix.astype(F32), jnp.zeros((63,), F32)]
        )[None]
        small = jnp.concatenate([small, swap_across(small)])
        small = jnp.concatenate([small, swap_core(small)])
        gain_attn_all, gain_mlp_all, b_down_all = (
            small[:, i * width : (i + 1) * width].reshape(-1) for i in range(3)
        )
        b_up_all = jnp.concatenate([b_up, swap_row(b_up)])
        sequence = row * across + place[0]
        away = col ^ sequence
        prefix_here = small[(away % 2) * 2 + away // 2, 3 * width].astype(jnp.int32)
        scalars = jnp.stack([prefix_here, core])

        x = spread(tokens, place)
        w1 = gather(w_qkv.reshape(width, block_cols))
        w2 = gather(jnp.concatenate([w_out.T, w_up, w_down.T], axis=1))
        grad_low = spread(cotangent, place)
        w_out_t, w_up_all, w_down_t = (
            jnp.concatenate(
                [
                    w2[:, r * 3 * hidden_width + i * hidden_width :][:, :hidden_width]
                    for r in range(rows)
                ],
                axis=1,
            )
            for i in range(3)
        )

        xf = x.astype(F32)
        r1 = lax.rsqrt(jnp.mean(xf * xf, axis=1, keepdims=True) + EPS)
        n1 = (xf * r1 * gain_attn_all).astype(BF)
        factor = QK_BASE / math.sqrt(HD) * jax.nn.softplus(query_scale)
        scaling = jnp.tile(
            jnp.concatenate([factor, jnp.ones((2 * HD,), F32)]), (rows * block_cols) // (3 * HD)
        )
        mixed = (dot(w1, n1, 0, 1) * scaling[:, None]).astype(BF)
        own = take(mixed, core, block_cols)
        other = swap_core(take(mixed, 1 - core, block_cols))
        o_own, o_other, mass = attend(scalars, own, other)
        o_back = swap_core(o_other)

        def in_order(mine, others):
            return jnp.where(
                core == 0, jnp.concatenate([mine, others]), jnp.concatenate([others, mine])
            )

        attended = in_order(o_own, o_back)
        middle = xf + dot(attended, w_out_t, 0, 1)
        r2 = lax.rsqrt(jnp.mean(middle * middle, axis=1, keepdims=True) + EPS)
        n2 = (middle * r2 * gain_mlp_all).astype(BF)
        before = dot(n2, w_up_all, 1, 0) + b_up_all
        gate = jax.nn.sigmoid(before)
        hidden = (before * gate).astype(BF)
        result = middle + dot(hidden, w_down_t, 1, 1) + b_down_all
        output = collect(result.astype(BF), place)

        grad = grad_low.astype(F32)
        d_b_down = jnp.sum(grad, axis=0)
        d_before = (
            dot(grad_low, w_down_t, 1, 0) * gate * (1.0 + before * (1.0 - gate))
        ).astype(BF)
        d_b_up = jnp.sum(d_before.astype(F32), axis=0)
        d_n2 = dot(d_before, w_up_all, 1, 1)
        d_gain_mlp = jnp.sum(d_n2 * middle * r2, axis=0)
        u2 = d_n2 * gain_mlp_all
        d_middle = (
            grad + r2 * u2 - middle * (r2 * r2 * r2 * jnp.mean(u2 * middle, axis=1, keepdims=True))
        )
        gm = d_middle.astype(BF)
        d_att = dot(w_out_t, gm, 0, 1).astype(BF)
        g_own = take(d_att, core, hidden_width)
        g_other = swap_core(take(d_att, 1 - core, hidden_width))

        half = across * width

        def grads_of(part):
            pieces = (
                dot(gm[:, part], attended, 0, 1, BF),
                dot(n2[:, part], d_before, 0, 0, BF),
                dot(grad_low[:, part], hidden, 0, 0, BF),
            )
            return jnp.concatenate(
                [
                    piece[:, r * hidden_width : (r + 1) * hidden_width]
                    for r in range(rows)
                    for piece in pieces
                ],
                axis=1,
            )

        near, far = slice(None, half), slice(half, None)
        d_w2 = scatter(grads_of(near), grads_of(far))
        d_own, d_other, d_factor = attend_back(
            scalars, factor[:, None], own, other, o_own, o_other, g_own, g_other, mass
        )
        d_mixed = in_order(d_own, swap_core(d_other))
        d_w1 = scatter(dot(n1[:, near], d_mixed, 0, 1, BF), dot(n1[:, far], d_mixed, 0, 1, BF))
        d_n1 = dot(d_mixed, w1, 0, 1)
        d_gain_attn = jnp.sum(d_n1 * xf * r1, axis=0)
        u1 = d_n1 * gain_attn_all
        d_x = d_middle + r1 * u1 - xf * (r1 * r1 * r1 * jnp.mean(u1 * xf, axis=1, keepdims=True))
        d_tokens = collect(d_x.astype(BF), place).astype(F32)

        d_factor = jnp.sum(d_factor.reshape(-1, HD, 128), axis=(0, 2)) / factor
        d_query_scale = d_factor * (QK_BASE / math.sqrt(HD)) * jax.nn.sigmoid(query_scale)

        by_col = jnp.stack([d_gain_attn, d_gain_mlp, d_b_down]).reshape(3, cols, width)
        owners = col ^ jnp.arange(cols)
        by_col = jnp.take(by_col, (owners % 2) * 2 + owners // 2, axis=1)
        by_row = d_b_up.reshape(rows, hidden_width)
        by_row = jnp.take(by_row, row ^ jnp.arange(rows), axis=0)
        packed = jnp.concatenate([by_col.reshape(-1), by_row.reshape(-1), d_query_scale])
        packed = lax.psum(packed, ("batch", "row", "col"))
        by_col = packed[: 3 * cols * width].reshape(3, cols, width)
        by_col = lax.dynamic_index_in_dim(by_col, col, 1, False)
        by_row = take(packed[3 * cols * width :], row, hidden_width)

        d_w1 = lax.psum(d_w1.astype(BF), "batch").astype(F32)
        d_w2 = lax.psum(d_w2.astype(BF), "batch").astype(F32)
        return (
            output,
            d_tokens,
            by_col[0],
            d_w1.reshape(w_qkv.shape),
            packed[-HD:],
            d_w2[:, :hidden_width].T,
            by_col[1],
            d_w2[:, hidden_width : 2 * hidden_width],
            by_row,
            d_w2[:, 2 * hidden_width :].T,
            by_col[2],
        )

    return shards


def gather_rows(portion):
    return lax.all_gather(portion, "row", axis=0, tiled=True)


def gather_cols(portion):
    return lax.all_gather(portion, "col", axis=0, tiled=True)


def term_maker(gathered, weight, transposed):
    if transposed:
        return lax.dot_general(
            gathered, weight, (((1,), (1,)), ((), ())), preferred_element_type=jnp.float32
        )
    return jnp.dot(gathered, weight, preferred_element_type=jnp.float32)


def sum_cols(gathered, weight, transposed):
    return lax.psum_scatter(
        term_maker(gathered, weight, transposed), "col", scatter_dimension=0, tiled=True
    )


def sum_rows(gathered, weight, transposed):
    return lax.psum_scatter(
        term_maker(gathered, weight, transposed), "row", scatter_dimension=0, tiled=True
    )


def across_cols(totals):
    return lax.psum(totals, "col")


def contract_rows(left_side, right_side):
    return lax.dot_general(
        left_side, right_side, (((0,), (0,)), ((), ())), preferred_element_type=jnp.float32
    )


def norm_scale(values):
    statistic = across_cols(jnp.sum(values * values, axis=1)) / D
    return lax.rsqrt(statistic + EPS)


def norm_back(d_normed, values, scaling, norm_gain):
    weighted = d_normed * norm_gain
    projected = across_cols(jnp.sum(weighted * values, axis=1)) / D
    d_values = (
        scaling[:, None] * weighted - values * (scaling * scaling * scaling * projected)[:, None]
    )
    d_gain = jnp.sum(d_normed * values * scaling[:, None], axis=0)
    return (d_values, d_gain)


def split_sequences(stacked, seq_count):
    return stacked.reshape(seq_count, -1, stacked.shape[-2], stacked.shape[-1])


def visible_mask(length, prefix_len):
    position = jnp.arange(length)
    return (position[None, :] < prefix_len) | (position[None, :] <= position[:, None])


def masked_scores(queries, key_rows, prefix_len):
    scores = jnp.einsum("qhd,khd->hqk", queries, key_rows, preferred_element_type=jnp.float32)
    return jnp.where(visible_mask(queries.shape[0], prefix_len)[None], scores, MASKED)


def attend_forward(pieces):
    queries, key_rows, values, prefix_len = pieces
    scores = masked_scores(queries, key_rows, prefix_len)
    highest = jnp.max(scores, axis=-1, keepdims=True)
    unscaled = jnp.exp(scores - highest)
    total_mass = jnp.sum(unscaled, axis=-1, keepdims=True)
    attn_probs = (unscaled / total_mass).astype(jnp.bfloat16)
    outcome = jnp.einsum("hqk,khd->qhd", attn_probs, values, preferred_element_type=jnp.float32)
    return (outcome.astype(jnp.bfloat16), highest[..., 0] + jnp.log(total_mass[..., 0]))


def attend_backward(pieces):
    queries, key_rows, values, d_outcome, log_mass, prefix_len = pieces
    scores = masked_scores(queries, key_rows, prefix_len)
    attn_probs = jnp.exp(scores - log_mass[..., None])
    d_values = jnp.einsum(
        "hqk,qhd->khd",
        attn_probs.astype(jnp.bfloat16),
        d_outcome,
        preferred_element_type=jnp.float32,
    ).astype(jnp.bfloat16)
    d_probs = jnp.einsum("qhd,khd->hqk", d_outcome, values, preferred_element_type=jnp.float32)
    centred = jnp.sum(attn_probs * d_probs, axis=-1, keepdims=True)
    d_scores = (attn_probs * (d_probs - centred)).astype(jnp.bfloat16)
    d_queries = jnp.einsum("hqk,khd->qhd", d_scores, key_rows, preferred_element_type=jnp.float32)
    d_keys = jnp.einsum(
        "hqk,qhd->khd", d_scores, queries, preferred_element_type=jnp.float32
    ).astype(jnp.bfloat16)
    return (d_queries, d_keys, d_values)


def forward(
    tokens, prefix, gain_attn, w_qkv, query_scale, w_out, gain_mlp, w_up, b_up, w_down, b_down
):
    block_rows = tokens.astype(jnp.float32)
    scale_attn = norm_scale(block_rows)
    normed_attn = (block_rows * scale_attn[:, None] * gain_attn).astype(jnp.bfloat16)
    whole_attn = gather_rows(normed_attn)
    head_count = w_qkv.shape[1]
    seq_count = prefix.shape[0]
    mixed_heads = sum_cols(whole_attn, w_qkv.reshape(w_qkv.shape[0], -1), False).reshape(
        -1, head_count, 3, HD
    )
    raw_queries = mixed_heads[:, :, 0]
    factor = QK_BASE / math.sqrt(HD) * jax.nn.softplus(query_scale)
    queries = (raw_queries * factor).astype(jnp.bfloat16)
    key_rows = mixed_heads[:, :, 1].astype(jnp.bfloat16)
    values = mixed_heads[:, :, 2].astype(jnp.bfloat16)
    outcome, log_mass = lax.map(
        attend_forward,
        (
            split_sequences(queries, seq_count),
            split_sequences(key_rows, seq_count),
            split_sequences(values, seq_count),
            prefix,
        ),
    )
    attended = outcome.reshape(-1, head_count * HD)
    whole_heads = gather_cols(attended)
    middle = block_rows + sum_rows(whole_heads, w_out, False)
    scale_mlp = norm_scale(middle)
    normed_mlp = (middle * scale_mlp[:, None] * gain_mlp).astype(jnp.bfloat16)
    whole_mlp = gather_rows(normed_mlp)
    before = sum_cols(whole_mlp, w_up, False) + b_up
    hidden = jax.nn.silu(before).astype(jnp.bfloat16)
    whole_hidden = gather_cols(hidden)
    result = middle + sum_rows(whole_hidden, w_down, False) + b_down
    saved_state = (
        scale_attn,
        whole_attn,
        raw_queries,
        queries,
        key_rows,
        values,
        log_mass,
        whole_heads,
        middle,
        scale_mlp,
        whole_mlp,
        before,
        whole_hidden,
        factor,
    )
    return (result, saved_state)


def spread_out(vector, length, slot_index):
    return lax.dynamic_update_slice(
        jnp.zeros((length,), jnp.float32), vector, (slot_index * vector.shape[0],)
    )


def take_own(vector, slot_index, slot_width):
    return lax.dynamic_slice(vector, (slot_index * slot_width,), (slot_width,))


def shards(
    tokens,
    prefix,
    gain_attn,
    w_qkv,
    query_scale,
    w_out,
    gain_mlp,
    w_up,
    b_up,
    w_down,
    b_down,
    cotangent,
):
    result, saved_state = forward(
        tokens, prefix, gain_attn, w_qkv, query_scale, w_out, gain_mlp, w_up, b_up, w_down, b_down
    )
    fresh_inputs = lax.optimization_barrier(
        (
            (
                tokens,
                prefix,
                gain_attn,
                w_qkv,
                query_scale,
                w_out,
                gain_mlp,
                w_up,
                b_up,
                w_down,
                b_down,
            ),
            result,
        )
    )[0]
    saved_state = forward(
        fresh_inputs[0],
        fresh_inputs[1],
        fresh_inputs[2],
        fresh_inputs[3],
        fresh_inputs[4],
        fresh_inputs[5],
        fresh_inputs[6],
        fresh_inputs[7],
        fresh_inputs[8],
        fresh_inputs[9],
        fresh_inputs[10],
    )[1]
    (
        scale_attn,
        whole_attn,
        raw_queries,
        queries,
        key_rows,
        values,
        log_mass,
        whole_heads,
        middle,
        scale_mlp,
        whole_mlp,
        before,
        whole_hidden,
        factor,
    ) = saved_state
    head_count = w_qkv.shape[1]
    seq_count = prefix.shape[0]
    grad_out = cotangent.astype(jnp.float32)
    whole_grad = gather_rows(cotangent)
    d_down = contract_rows(whole_hidden, whole_grad)
    d_hidden = sum_cols(whole_grad, w_down, True)
    gate_sig = jax.nn.sigmoid(before)
    d_before = (d_hidden * gate_sig * (1.0 + before * (1.0 - gate_sig))).astype(jnp.bfloat16)
    whole_before = gather_cols(d_before)
    d_up = contract_rows(whole_mlp, whole_before)
    d_normed_mlp = sum_rows(whole_before, w_up, True)
    d_middle_norm, d_gain_mlp = norm_back(d_normed_mlp, middle, scale_mlp, gain_mlp)
    d_middle = grad_out + d_middle_norm
    whole_middle = gather_rows(d_middle.astype(jnp.bfloat16))
    d_out = contract_rows(whole_heads, whole_middle)
    d_attended = (
        sum_cols(whole_middle, w_out, True).astype(jnp.bfloat16).reshape(-1, head_count, HD)
    )
    d_queries, d_keys, d_values = lax.map(
        attend_backward,
        (
            split_sequences(queries, seq_count),
            split_sequences(key_rows, seq_count),
            split_sequences(values, seq_count),
            split_sequences(d_attended, seq_count),
            log_mass,
            prefix,
        ),
    )
    d_queries = d_queries.reshape(-1, head_count, HD)
    d_factor = jnp.sum(d_queries * raw_queries, axis=(0, 1))
    d_query_scale = d_factor * (QK_BASE / math.sqrt(HD)) * jax.nn.sigmoid(query_scale)
    d_mixed = jnp.stack(
        [
            (d_queries * factor).astype(jnp.bfloat16),
            d_keys.reshape(-1, head_count, HD),
            d_values.reshape(-1, head_count, HD),
        ],
        axis=2,
    ).reshape(d_queries.shape[0], -1)
    whole_mixed = gather_cols(d_mixed)
    d_qkv = contract_rows(whole_attn, whole_mixed)
    d_normed_attn = sum_rows(whole_mixed, w_qkv.reshape(w_qkv.shape[0], -1), True)
    d_rows_norm, d_gain_attn = norm_back(
        d_normed_attn, tokens.astype(jnp.float32), scale_attn, gain_attn
    )
    d_tokens = d_middle + d_rows_norm
    col_index = lax.axis_index("col")
    row_index = lax.axis_index("row")
    d_b_up = jnp.sum(d_before.astype(jnp.float32), axis=0)
    d_b_down = jnp.sum(grad_out, axis=0)
    smalls = lax.psum(
        (
            spread_out(d_gain_attn, D, col_index),
            spread_out(d_gain_mlp, D, col_index),
            spread_out(d_b_up, FF, row_index),
            spread_out(d_b_down, D, col_index),
            d_query_scale,
        ),
        ("batch", "row", "col"),
    )
    weights = lax.psum((d_qkv, d_out, d_up, d_down), "batch")
    feature_width = gain_attn.shape[0]
    return (
        result.astype(jnp.bfloat16),
        d_tokens,
        take_own(smalls[0], col_index, feature_width),
        weights[0].reshape(w_qkv.shape),
        smalls[4],
        weights[1],
        take_own(smalls[1], col_index, feature_width),
        weights[2],
        take_own(smalls[2], row_index, b_up.shape[0]),
        weights[3],
        take_own(smalls[3], col_index, feature_width),
    )


def solution(mesh):
    in_specs = (
        P(("batch", "row"), "col"),
        P(("batch", "col")),
        P("col"),
        P("col", "row", None),
        P(),
        P("row", "col"),
        P("col"),
        P("col", "row"),
        P("row"),
        P("row", "col"),
        P("col"),
        P(("batch", "row"), "col"),
    )
    out_specs = (
        P(("batch", "row"), "col"),
        P(("batch", "row"), "col"),
        P("col"),
        P("col", "row", None),
        P(),
        P("row", "col"),
        P("col"),
        P("col", "row"),
        P("row"),
        P("row", "col"),
        P("col"),
    )
    shape = dict(mesh.shape)
    by_weights = shape["row"] == 2 and shape["col"] == 4
    plan = gathered_plan(shape["row"], shape["col"]) if by_weights else shards
    return jax.shard_map(plan, mesh=mesh, in_specs=in_specs, out_specs=out_specs, check_vma=False)
```

```python
import math

import jax
import jax.numpy as jnp
from jax import lax
from jax.experimental import pallas as pl
from jax.experimental.pallas import tpu as pltpu
from jax.sharding import PartitionSpec as P

D = 1280
FF = 1280
HD = 80


QK_BASE = 1.442695041
EPS = 1e-06
MASKED = -1e30
LOG2E = 1.4426950408889634


BF = jnp.bfloat16
F32 = jnp.float32


def dot(left, right, left_dim, right_dim, kind=F32):
    return lax.dot_general(
        left, right, (((left_dim,), (right_dim,)), ((), ())), preferred_element_type=kind
    )


def swap(values, axis, bit, size):
    return lax.ppermute(values, axis, [(i, i ^ bit) for i in range(size)])


def _tiles(length):
    return max(length // 4, 128)


def _visible(scores, key_start, query_start, prefix):
    keys = key_start + lax.broadcasted_iota(jnp.int32, scores.shape, 0)
    queries = query_start + lax.broadcasted_iota(jnp.int32, scores.shape, 1)
    return jnp.where((keys < prefix) | (keys <= queries), scores, MASKED)


def _join(buffer, own_ref, other_ref, core, width):
    buffer[:, pl.ds(pl.multiple_of(core * width, 128), width)] = own_ref[...]
    buffer[:, pl.ds(pl.multiple_of((1 - core) * width, 128), width)] = other_ref[...]


def _split(buffer, own_ref, other_ref, core, width):
    own_ref[...] = buffer[:, pl.ds(pl.multiple_of(core * width, 128), width)]
    other_ref[...] = buffer[:, pl.ds(pl.multiple_of((1 - core) * width, 128), width)]


def attend_kernel(scalars, own_ref, other_ref, o_own_ref, o_other_ref, mass_ref, qkv, out):
    prefix, core = scalars[0], scalars[1]
    width = own_ref.shape[1]
    length = 2 * width
    tile = _tiles(length)
    _join(qkv, own_ref, other_ref, core, width)
    keys = qkv[HD : 2 * HD, :].T
    for start in range(0, length, tile):
        reach = max(start + tile, length // 2)
        scores = dot(keys[:reach], qkv[:HD, start : start + tile], 1, 0)
        low = 0 if start < length // 2 else start
        masked = _visible(scores[low:reach], low, start, prefix)
        scores = masked if low == 0 else jnp.concatenate([scores[:low], masked], axis=0)
        highest = jnp.max(scores, axis=0, keepdims=True) * LOG2E
        unscaled = jnp.exp2(scores * LOG2E - highest)
        total = jnp.sum(unscaled, axis=0, keepdims=True)
        probs = (unscaled * (1.0 / total)).astype(BF)
        out[:, start : start + tile] = dot(qkv[2 * HD :, :reach], probs, 1, 0).astype(BF)
        mass_ref[:, start : start + tile] = highest + jnp.log(total) * LOG2E
    _split(out, o_own_ref, o_other_ref, core, width)


def attend_back_kernel(
    scalars, factor_ref, own_ref, other_ref, o_own_ref, o_other_ref, g_own_ref, g_other_ref, mass_ref,
    d_own_ref, d_other_ref, d_factor_ref, qkv, out, grad, d_qkv, d_keys, d_values,
):
    prefix, core = scalars[0], scalars[1]
    width = own_ref.shape[1]
    length = 2 * width
    tile = _tiles(length)
    _join(qkv, own_ref, other_ref, core, width)
    _join(out, o_own_ref, o_other_ref, core, width)
    _join(grad, g_own_ref, g_other_ref, core, width)
    queries = qkv[:HD, :].T
    keys = qkv[HD : 2 * HD, :].T
    values = qkv[2 * HD :, :].T
    grads = grad[...].T
    d_keys[...] = jnp.zeros_like(d_keys)
    d_values[...] = jnp.zeros_like(d_values)
    d_factor = jnp.zeros((HD, 128), F32)
    for start in range(0, length, tile):
        reach = max(start + tile, length // 2)
        here = slice(start, start + tile)
        scores = dot(keys[:reach], qkv[:HD, here], 1, 0)
        low = 0 if start < length // 2 else start
        masked = _visible(scores[low:reach], low, start, prefix)
        scores = masked if low == 0 else jnp.concatenate([scores[:low], masked], axis=0)
        probs = jnp.exp2(scores * LOG2E - mass_ref[:, here])
        d_values[:reach] += dot(probs.astype(BF), grads[here], 1, 0)
        d_probs = dot(values[:reach], grad[:, here], 1, 0)
        centre = jnp.sum(grad[:, here].astype(F32) * out[:, here].astype(F32), axis=0, keepdims=True)
        d_scores = (probs * (d_probs - centre)).astype(BF)
        d_keys[:reach] += dot(d_scores, queries[here], 1, 0)
        d_queries = dot(qkv[HD : 2 * HD, :reach], d_scores, 1, 0)
        product = d_queries * qkv[:HD, here].astype(F32)
        for lane in range(0, tile, 128):
            d_factor = d_factor + product[:, lane : lane + 128]
        d_qkv[:HD, here] = (d_queries * factor_ref[...]).astype(BF)
    d_factor_ref[...] = d_factor
    d_qkv[HD : 2 * HD, :] = d_keys[...].T.astype(BF)
    d_qkv[2 * HD :, :] = d_values[...].T.astype(BF)
    _split(d_qkv, d_own_ref, d_other_ref, core, width)


def _head(rows, width, first=0):
    return pl.BlockSpec((rows, width), lambda h, s: (h + first if first else h, 0))


def attend(scalars, own, other, first, heads):
    width = own.shape[1]
    length = 2 * width
    return pl.pallas_call(
        attend_kernel,
        grid_spec=pltpu.PrefetchScalarGridSpec(
            num_scalar_prefetch=1,
            grid=(heads,),
            in_specs=[_head(3 * HD, width, first)] * 2,
            out_specs=[_head(HD, width)] * 2
            + [pl.BlockSpec((None, 1, length), lambda h, s: (h, 0, 0))],
            scratch_shapes=[pltpu.VMEM((3 * HD, length), BF), pltpu.VMEM((HD, length), BF)],
        ),
        out_shape=[jax.ShapeDtypeStruct((heads * HD, width), BF)] * 2
        + [jax.ShapeDtypeStruct((heads, 1, length), F32)],
        cost_estimate=pl.CostEstimate(
            flops=24 * heads * length * length * 128,
            bytes_accessed=4 * heads * length * 4 * HD,
            transcendentals=heads * length * length,
        ),
        name="attend",
    )(scalars, own, other)


def attend_back(
    scalars, factor, own, other, o_own, o_other, g_own, g_other, mass, first, heads
):
    width = own.shape[1]
    length = 2 * width
    return pl.pallas_call(
        attend_back_kernel,
        grid_spec=pltpu.PrefetchScalarGridSpec(
            num_scalar_prefetch=1,
            grid=(heads,),
            in_specs=[pl.BlockSpec((HD, 1), lambda h, s: (0, 0))]
            + [_head(3 * HD, width, first)] * 2
            + [_head(HD, width)] * 2
            + [_head(HD, width, first)] * 2
            + [pl.BlockSpec((None, 1, length), lambda h, s: (h, 0, 0))],
            out_specs=[_head(3 * HD, width)] * 2 + [_head(HD, 128)],
            scratch_shapes=[
                pltpu.VMEM((3 * HD, length), BF),
                pltpu.VMEM((HD, length), BF),
                pltpu.VMEM((HD, length), BF),
                pltpu.VMEM((3 * HD, length), BF),
                pltpu.VMEM((length, HD), F32),
                pltpu.VMEM((length, HD), F32),
            ],
        ),
        out_shape=[jax.ShapeDtypeStruct((heads * 3 * HD, width), BF)] * 2
        + [jax.ShapeDtypeStruct((heads * HD, 128), F32)],
        cost_estimate=pl.CostEstimate(
            flops=26 * heads * length * length * 128,
            bytes_accessed=4 * heads * length * 10 * HD,
            transcendentals=heads * length * length,
        ),
        name="attend_back",
    )(scalars, factor, own, other, o_own, o_other, g_own, g_other, mass)


def block_places(height, cut):
    places = [(0, 0), (height, 0), (0, 1), (height, 1), (height + cut, 1)]
    return places + [(2 * height + start, r) for start, r in places]


def project_kernel(core_ref, x0, x1, x2, x3, gain, scaling, *refs):
    pieces, (n1_ref, x_ref, r1_ref, own_ref, other_ref, whole_ref, whole, sems) = refs[:10], refs[10:]
    core = core_ref[0]
    height, width = pieces[0].shape
    columns = width
    copies = []
    for i, piece in enumerate(pieces):
        start, r = block_places(height, pieces[3].shape[0])[i]
        copies.append(
            pltpu.make_async_copy(
                piece,
                whole.at[pl.ds(start, piece.shape[0]), pl.ds(r * columns, columns)],
                sems.at[i],
            )
        )
    for copy in copies:
        copy.start()
    xs = [ref[...].astype(F32) for ref in (x0, x1, x2, x3)]
    total = sum(jnp.sum(v * v, axis=0, keepdims=True) for v in xs)
    r1 = lax.rsqrt(total / (4 * height) + EPS)
    r1_ref[...] = r1
    for i, v in enumerate(xs):
        rows_here = pl.ds(i * height, height)
        x_ref[rows_here, :] = v.astype(BF)
        n1_ref[rows_here, :] = (v * r1 * gain[rows_here, :]).astype(BF)
    for copy in copies:
        copy.wait()
    out = pltpu.make_async_copy(whole, whole_ref, sems.at[10])
    out.start()
    tile = columns // 3
    for ref, r in ((other_ref, 1 - core), (own_ref, core)):
        for j in range(3):
            block = whole[:, pl.ds(pl.multiple_of(r * columns + j * tile, 128), tile)]
            term = dot(block, n1_ref[...], 0, 0)
            here = slice(j * tile, (j + 1) * tile)
            ref[here, :] = (term * scaling[here, :]).astype(BF)
    out.wait()


def project(core, x_blocks, gain, scaling, pieces):
    height, width = pieces[0].shape
    count = x_blocks[0].shape[1]
    vmem, anywhere = pl.BlockSpec(memory_space=pltpu.VMEM), pl.BlockSpec(memory_space=pl.ANY)
    return pl.pallas_call(
        project_kernel,
        in_specs=[pl.BlockSpec(memory_space=pltpu.SMEM)] + [vmem] * 6 + [anywhere] * 10,
        out_specs=[vmem] * 5 + [anywhere],
        out_shape=[
            jax.ShapeDtypeStruct((4 * height, count), BF),
            jax.ShapeDtypeStruct((4 * height, count), BF),
            jax.ShapeDtypeStruct((1, count), F32),
            jax.ShapeDtypeStruct((width, count), BF),
            jax.ShapeDtypeStruct((width, count), BF),
            jax.ShapeDtypeStruct((4 * height, 2 * width), BF),
        ],
        scratch_shapes=[
            pltpu.VMEM((4 * height, 2 * width), BF),
            pltpu.SemaphoreType.DMA((11,)),
        ],
        cost_estimate=pl.CostEstimate(
            flops=16 * height * width * count,
            bytes_accessed=16 * height * width,
            transcendentals=0,
        ),
        name="project",
    )(core, *x_blocks, gain, scaling, *pieces)


def assemble_kernel(core_ref, *refs):
    blocks, own, back = refs[:10], refs[10:12], refs[12:14]
    wholes, attended, sems = refs[14:17], refs[17], refs[18]
    height, width = blocks[0].shape[0], blocks[0].shape[1] // 3
    pairs = []
    for b, block in enumerate(blocks):
        start, r = block_places(height, blocks[3].shape[0])[b]
        for i, whole in enumerate(wholes):
            pairs.append(
                (
                    block.at[:, pl.ds(i * width, width)],
                    whole.at[pl.ds(start, block.shape[0]), pl.ds(r * width, width)],
                )
            )
    for parts, r in ((own, core_ref[0]), (back, 1 - core_ref[0])):
        start = 0
        for part in parts:
            here = pl.ds(pl.multiple_of(r * width + start, 16), part.shape[0])
            pairs.append((part, attended.at[here]))
            start += part.shape[0]
    copies = [pltpu.make_async_copy(a, b, sems.at[i]) for i, (a, b) in enumerate(pairs)]
    for copy in copies:
        copy.start()
    for copy in copies:
        copy.wait()


def assemble(core, blocks, own, back):
    height, width = blocks[0].shape[0], blocks[0].shape[1] // 3
    count = own[0].shape[1]
    shape = jax.ShapeDtypeStruct((4 * height, 2 * width), BF)
    return pl.pallas_call(
        assemble_kernel,
        in_specs=[pl.BlockSpec(memory_space=pltpu.SMEM)] + [pl.BlockSpec(memory_space=pl.ANY)] * 14,
        out_specs=[pl.BlockSpec(memory_space=pltpu.VMEM)] * 4,
        out_shape=[shape] * 3
        + [jax.ShapeDtypeStruct((2 * width, count), BF)],
        scratch_shapes=[pltpu.SemaphoreType.DMA((34,))],
        cost_estimate=pl.CostEstimate(
            flops=0, bytes_accessed=4 * 4 * height * 6 * width, transcendentals=0
        ),
        name="assemble",
    )(core, *blocks, *own, *back)


def finish_kernel(
    w_ref, d_first, d_second, gain, x_ref, r1_ref, d_middle_ref, d_x_ref, d_gain_ref, total, d_mixed
):
    step = pl.program_id(0)
    height = w_ref.shape[0]

    @pl.when(step == 0)
    def _():
        size = d_first.shape[0] // 2
        for i in range(4):
            source = (d_first, d_second)[i % 2]
            d_mixed[i * size : (i + 1) * size, :] = source[(i // 2) * size : (i // 2 + 1) * size, :]

    term = dot(w_ref[...], d_mixed[...], 1, 0)
    total[pl.ds(pl.multiple_of(step * height, height), height), :] = term

    @pl.when(step == pl.num_programs(0) - 1)
    def _():
        r1 = r1_ref[...]
        count = x_ref.shape[0]
        projected = jnp.zeros_like(r1)
        for i in range(0, count, height):
            here = slice(i, i + height)
            product = total[here, :] * x_ref[here, :].astype(F32)
            projected += jnp.sum(product * gain[here, :], axis=0, keepdims=True)
            d_gain_ref[here, :] = jnp.sum(product * r1, axis=1, keepdims=True)
        projected = r1 * r1 * r1 * (projected / count)
        for i in range(0, count, height):
            here = slice(i, i + height)
            x = x_ref[here, :].astype(F32)
            d_x = d_middle_ref[here, :] + r1 * (total[here, :] * gain[here, :]) - x * projected
            d_x_ref[here, :] = d_x.astype(BF)


def finish(w, d_mixed, gain, x, r1, d_middle):
    count, width = x.shape
    height = count // 4

    def whole(v):
        return pl.BlockSpec(v.shape, lambda i: (0, 0))

    rest = (*d_mixed, gain, x, r1, d_middle)
    return pl.pallas_call(
        finish_kernel,
        grid=(4,),
        in_specs=[pl.BlockSpec((height, w.shape[1]), lambda i: (i, 0))] + [whole(v) for v in rest],
        out_specs=[whole(x), whole(gain)],
        out_shape=[
            jax.ShapeDtypeStruct((count, width), BF),
            jax.ShapeDtypeStruct((count, 1), F32),
        ],
        scratch_shapes=[pltpu.VMEM((count, width), F32), pltpu.VMEM((w.shape[1], width), BF)],
        cost_estimate=pl.CostEstimate(
            flops=4 * count * w.shape[1] * width, bytes_accessed=2 * w.size, transcendentals=0
        ),
        name="finish",
    )(w, *rest)


def after(value, *others):
    return lax.optimization_barrier((value, *others))[0]


def gathered_plan(batches, rows, cols):
    across = cols // 2

    def swap_core(v):
        return swap(v, "col", 1, cols)

    def swap_across(v):
        return swap(v, "col", 2, cols)

    def swap_row(v):
        return swap(v, "row", 1, rows)

    def part(v, index, width, axis=1):
        return lax.dynamic_slice_in_dim(v, index * width, width, axis)

    def choose(test, a, b):
        return jnp.where(test, a, b), jnp.where(test, b, a)

    def spread(block, place):
        x, core = place
        height, count = block.shape[0], block.shape[1] // cols
        away = swap_across(part(block, 1 - x, 2 * count))
        near = part(block, 2 * x + core, count)
        near_away = part(away, core, count)
        far = jnp.concatenate([part(block, 2 * x + 1 - core, count), part(away, 1 - core, count)])
        far = swap_core(far)
        return [near, near_away, far[:height], far[height:]]

    def collect(whole, place, kind):
        x, core = place
        height, count = whole.shape[0] // 4, whole.shape[1]
        far = swap_core(whole[2 * height :])
        away = jnp.concatenate([whole[height : 2 * height], far[height:]])
        away = swap_across(away)
        tokens = jnp.zeros((height, cols * count), kind)
        for v, place_of in (
            (whole[:height], 2 * x + core),
            (far[:height], 2 * x + 1 - core),
            (away[:height], 2 * (1 - x) + core),
            (away[height:], 2 * (1 - x) + 1 - core),
        ):
            tokens = lax.dynamic_update_slice(tokens, v.astype(kind), (0, place_of * count))
        return tokens.T

    def wide(*values):
        return sum(v.astype(F32) for v in values).astype(BF)

    def scatter_row(total):
        width, height = total.shape[1] // 2, total.shape[0] // 2
        got = swap_row(total[:, width:])
        last = swap_across(wide(total[height:, :width], got[height:]))
        return wide(total[:height, :width], got[:height], last)

    def scatter_both(total):
        width, height = total.shape[1] // 2, total.shape[0] // 2
        half = height // 2
        first_x = swap_across(total[height : height + half])
        second_y = swap_row(
            jnp.concatenate([total[half:height, width:], total[height + half :, width:]]),
        )
        first_y = swap_row(wide(total[:half, width:], first_x[:, width:]))
        third = wide(total[height + half :, :width], second_y[half:])
        second_x = swap_across(third)
        result = jnp.concatenate(
            [
                wide(total[:half, :width], first_x[:, :width], first_y),
                wide(total[half:height, :width], second_y[:half], second_x),
            ]
        )
        return result, third

    def by_row_block(values):
        halves = [jnp.split(v, rows, axis=1) for v in values]
        return jnp.concatenate([h[r] for r in range(rows) for h in halves], axis=1)

    def sum_batches(v, inner):
        def move(v, pairs):
            return lax.ppermute(v, "batch", pairs)

        def add(v, got):
            return (v.astype(F32) + got.astype(F32)).astype(v.dtype)

        v = add(v, move(v, [(0, 1), (3, 2)]))
        v = add(v, move(v, [(1, 2), (2, 1)]))
        got = move(v, [(1, 0), (2, 3)])
        return jnp.where(inner, v, got).astype(F32)

    def shards(
        tokens, prefix, gain_attn, w_qkv, query_scale, w_out, gain_mlp, w_up, b_up, w_down, b_down, cotangent
    ):
        col, row, batch = lax.axis_index("col"), lax.axis_index("row"), lax.axis_index("batch")
        place = (col // 2, col % 2)
        core = place[1]
        first_core = core == 0
        inner = (batch == 1) | (batch == 2)
        width = gain_attn.shape[0]
        hidden_width = b_up.shape[0]
        heads = w_qkv.shape[1]
        block_cols = heads * w_qkv.shape[2]
        half = across * width
        split = heads // 2
        groups = ((0, split), (split, heads - split))

        x_blocks = spread(tokens.T, place)
        piece = w_qkv.reshape(width, block_cols)
        piece_y = swap_row(piece)
        piece_x = swap_across(piece)
        small = jnp.concatenate(
            [gain_attn, gain_mlp, b_down, prefix.astype(F32), jnp.zeros((63,), F32)]
        )[None]
        small = jnp.concatenate([small, swap_across(small)])
        small = jnp.concatenate([small, swap_core(small)])
        gain_attn_all, gain_mlp_all, b_down_all = (
            small[:, i * width : (i + 1) * width].reshape(-1, 1) for i in range(3)
        )
        b_up_all = jnp.concatenate([b_up, swap_row(b_up)])[:, None]
        sequence = row * across + place[0]
        away = col ^ sequence
        prefix_here = small[(away % 2) * 2 + away // 2, 3 * width].astype(jnp.int32)
        scalars = jnp.stack([prefix_here, core])
        cut = width // 2

        def whole_group(piece, piece_x, piece_y):
            pieces = [piece, piece_x, piece_y, swap_row(piece_x[:cut]), swap_across(piece_y[cut:])]
            return pieces + [swap_core(p) for p in pieces]

        pieces = whole_group(piece, piece_x, piece_y)

        low = jnp.concatenate([w_out.T, w_up, w_down.T], axis=1)
        low = after(low, piece_x, piece_y)
        low_y = swap_row(low)
        low_x = swap_across(low)
        g_blocks = spread(after(cotangent.T, low_x), place)
        low_pieces = whole_group(low, low_x, low_y)

        factor = QK_BASE / math.sqrt(HD) * jax.nn.softplus(query_scale)
        scaling = jnp.tile(jnp.concatenate([factor, jnp.ones((2 * HD,), F32)]), heads)[:, None]
        n1, x, r1, own, other, w1 = project(core[None], x_blocks, gain_attn_all, scaling, pieces)
        other = swap_core(other)
        xf = x.astype(F32)
        parts = []
        for first, number in groups:
            parts.append(attend(scalars, own, other, first, number))
        o_own = [p[0] for p in parts]
        o_other = [p[1] for p in parts]
        mass = [p[2] for p in parts]
        o_back = [swap_core(v) for v in o_other]
        w_out_t, w_up_all, w_down_t, attended = assemble(core[None], low_pieces, o_own, o_back)
        g = jnp.concatenate(g_blocks)
        middle = xf + dot(w_out_t, attended, 1, 0)
        r2 = lax.rsqrt(jnp.mean(middle * middle, axis=0, keepdims=True) + EPS)
        n2 = (middle * r2 * gain_mlp_all).astype(BF)
        before = dot(w_up_all, n2, 0, 0) + b_up_all
        gate = jax.nn.sigmoid(before)
        hidden = (before * gate).astype(BF)
        near, far = slice(None, half), slice(half, None)

        def gradient(left, right):
            send = swap_core(dot(left[far], right, 1, 1, BF))
            return (dot(left[near], right, 1, 1) + send.astype(F32)).astype(BF)

        d_w_down = gradient(g, hidden)
        result = (middle + dot(w_down_t, hidden, 1, 0) + b_down_all).astype(BF)

        grad = g.astype(F32)
        d_b_down = jnp.sum(grad, axis=1)
        d_before = (
            dot(w_down_t, g, 0, 0) * gate * (1.0 + before * (1.0 - gate))
        ).astype(BF)
        d_b_up = jnp.sum(d_before.astype(F32), axis=1)
        d_w_up = gradient(n2, d_before)
        d_mlp, _ = scatter_both(by_row_block([d_w_up, d_w_down]))
        d_n2 = dot(w_up_all, d_before, 1, 0)
        d_gain_mlp = jnp.sum(d_n2 * middle * r2, axis=1)
        u2 = d_n2 * gain_mlp_all
        d_middle = (
            grad + r2 * u2 - middle * (r2 * r2 * r2 * jnp.mean(u2 * middle, axis=0, keepdims=True))
        )
        gm = d_middle.astype(BF)
        d_att = dot(w_out_t, gm, 0, 0).astype(BF)
        g_own, g_other = choose(first_core, d_att[:hidden_width], d_att[hidden_width:])
        g_other = swap_core(g_other)
        d_w_out = scatter_row(gradient(gm, attended))
        output = collect(result, place, BF)

        backs = []
        for i, (first, number) in enumerate(groups):
            backs.append(
                attend_back(
                    scalars, factor[:, None], own, other, o_own[i], o_other[i], g_own, g_other,
                    mass[i], first, number,
                )
            )
        d_w1, d_mixed = [], []
        for i, (d_own, d_other, d_factor_part) in enumerate(backs):
            d_back = swap_core(d_other)
            if i:
                d_own, d_back = lax.optimization_barrier((d_own, d_back, total, third))[:2]
            d_mix = jnp.concatenate(choose(first_core, d_own, d_back))
            d_mixed.append(d_mix)
            total = gradient(n1, d_mix)
            summed, third = scatter_both(total)
            d_w1.append(summed)
        d_factor = sum(jnp.sum(p[2].reshape(-1, HD, 128), axis=(0, 2)) for p in backs) / factor
        d_mixed[-1] = after(d_mixed[-1], total)
        d_x, d_gain_attn = finish(w1, d_mixed, gain_attn_all, x, r1, d_middle)
        d_gain_attn = d_gain_attn[:, 0]
        d_tokens = collect(after(d_x, third), place, F32)

        d_query_scale = d_factor * (QK_BASE / math.sqrt(HD)) * jax.nn.sigmoid(query_scale)

        by_col = jnp.stack([d_gain_attn, d_gain_mlp, d_b_down]).reshape(3, cols * width)
        cb, rb, qs = by_col.reshape(3, 2, across, width), d_b_up.reshape(rows, hidden_width), d_query_scale

        def exchange(send, mover):
            flat = jnp.concatenate([v.reshape(-1) for v in send])
            got = mover(flat)
            out, at = [], 0
            for v in send:
                out.append(got[at : at + v.size].reshape(v.shape))
                at += v.size
            return out

        g_cb, g_rb, g_qs = exchange((cb[:, 1], rb, qs), lambda v: swap_core(v))
        cb, rb, qs = cb[:, 0] + g_cb, rb + g_rb, qs + g_qs
        g_cb, g_rb, g_qs = exchange((cb[:, 1], rb, qs), lambda v: swap_across(v))
        cb, rb, qs = cb[:, 0] + g_cb, rb + g_rb, qs + g_qs
        g_cb, g_rb, g_qs = exchange((cb, rb[1], qs), lambda v: swap_row(v))
        cb, rb, qs = cb + g_cb, rb[0] + g_rb, qs + g_qs
        flat = sum_batches(jnp.concatenate([cb.reshape(-1), rb, qs]), inner)
        cb = flat[: cb.size].reshape(cb.shape)
        rb, qs = flat[cb.size : -HD], flat[-HD:]

        d_mlp = sum_batches(d_mlp, inner)
        d_w_out = sum_batches(d_w_out, inner)
        d_w_up, d_w_down = d_mlp[:, :hidden_width], d_mlp[:, hidden_width:]
        d_w1 = jnp.concatenate([sum_batches(v, inner) for v in d_w1], axis=1)
        return (
            output,
            d_tokens,
            cb[0],
            d_w1.reshape(w_qkv.shape),
            qs,
            d_w_out.T,
            cb[1],
            d_w_up,
            rb,
            d_w_down.T,
            cb[2],
        )

    return shards


def gather_rows(portion):
    return lax.all_gather(portion, "row", axis=0, tiled=True)


def gather_cols(portion):
    return lax.all_gather(portion, "col", axis=0, tiled=True)


def term_maker(gathered, weight, transposed):
    if transposed:
        return lax.dot_general(
            gathered, weight, (((1,), (1,)), ((), ())), preferred_element_type=jnp.float32
        )
    return jnp.dot(gathered, weight, preferred_element_type=jnp.float32)


def sum_cols(gathered, weight, transposed):
    return lax.psum_scatter(
        term_maker(gathered, weight, transposed), "col", scatter_dimension=0, tiled=True
    )


def sum_rows(gathered, weight, transposed):
    return lax.psum_scatter(
        term_maker(gathered, weight, transposed), "row", scatter_dimension=0, tiled=True
    )


def across_cols(totals):
    return lax.psum(totals, "col")


def contract_rows(left_side, right_side):
    return lax.dot_general(
        left_side, right_side, (((0,), (0,)), ((), ())), preferred_element_type=jnp.float32
    )


def norm_scale(values):
    statistic = across_cols(jnp.sum(values * values, axis=1)) / D
    return lax.rsqrt(statistic + EPS)


def norm_back(d_normed, values, scaling, norm_gain):
    weighted = d_normed * norm_gain
    projected = across_cols(jnp.sum(weighted * values, axis=1)) / D
    d_values = (
        scaling[:, None] * weighted - values * (scaling * scaling * scaling * projected)[:, None]
    )
    d_gain = jnp.sum(d_normed * values * scaling[:, None], axis=0)
    return (d_values, d_gain)


def split_sequences(stacked, seq_count):
    return stacked.reshape(seq_count, -1, stacked.shape[-2], stacked.shape[-1])


def visible_mask(length, prefix_len):
    position = jnp.arange(length)
    return (position[None, :] < prefix_len) | (position[None, :] <= position[:, None])


def masked_scores(queries, key_rows, prefix_len):
    scores = jnp.einsum("qhd,khd->hqk", queries, key_rows, preferred_element_type=jnp.float32)
    return jnp.where(visible_mask(queries.shape[0], prefix_len)[None], scores, MASKED)


def attend_forward(pieces):
    queries, key_rows, values, prefix_len = pieces
    scores = masked_scores(queries, key_rows, prefix_len)
    highest = jnp.max(scores, axis=-1, keepdims=True)
    unscaled = jnp.exp(scores - highest)
    total_mass = jnp.sum(unscaled, axis=-1, keepdims=True)
    attn_probs = (unscaled / total_mass).astype(jnp.bfloat16)
    outcome = jnp.einsum("hqk,khd->qhd", attn_probs, values, preferred_element_type=jnp.float32)
    return (outcome.astype(jnp.bfloat16), highest[..., 0] + jnp.log(total_mass[..., 0]))


def attend_backward(pieces):
    queries, key_rows, values, d_outcome, log_mass, prefix_len = pieces
    scores = masked_scores(queries, key_rows, prefix_len)
    attn_probs = jnp.exp(scores - log_mass[..., None])
    d_values = jnp.einsum(
        "hqk,qhd->khd",
        attn_probs.astype(jnp.bfloat16),
        d_outcome,
        preferred_element_type=jnp.float32,
    ).astype(jnp.bfloat16)
    d_probs = jnp.einsum("qhd,khd->hqk", d_outcome, values, preferred_element_type=jnp.float32)
    centred = jnp.sum(attn_probs * d_probs, axis=-1, keepdims=True)
    d_scores = (attn_probs * (d_probs - centred)).astype(jnp.bfloat16)
    d_queries = jnp.einsum("hqk,khd->qhd", d_scores, key_rows, preferred_element_type=jnp.float32)
    d_keys = jnp.einsum(
        "hqk,qhd->khd", d_scores, queries, preferred_element_type=jnp.float32
    ).astype(jnp.bfloat16)
    return (d_queries, d_keys, d_values)


def forward(
    tokens, prefix, gain_attn, w_qkv, query_scale, w_out, gain_mlp, w_up, b_up, w_down, b_down
):
    block_rows = tokens.astype(jnp.float32)
    scale_attn = norm_scale(block_rows)
    normed_attn = (block_rows * scale_attn[:, None] * gain_attn).astype(jnp.bfloat16)
    whole_attn = gather_rows(normed_attn)
    head_count = w_qkv.shape[1]
    seq_count = prefix.shape[0]
    mixed_heads = sum_cols(whole_attn, w_qkv.reshape(w_qkv.shape[0], -1), False).reshape(
        -1, head_count, 3, HD
    )
    raw_queries = mixed_heads[:, :, 0]
    factor = QK_BASE / math.sqrt(HD) * jax.nn.softplus(query_scale)
    queries = (raw_queries * factor).astype(jnp.bfloat16)
    key_rows = mixed_heads[:, :, 1].astype(jnp.bfloat16)
    values = mixed_heads[:, :, 2].astype(jnp.bfloat16)
    outcome, log_mass = lax.map(
        attend_forward,
        (
            split_sequences(queries, seq_count),
            split_sequences(key_rows, seq_count),
            split_sequences(values, seq_count),
            prefix,
        ),
    )
    attended = outcome.reshape(-1, head_count * HD)
    whole_heads = gather_cols(attended)
    middle = block_rows + sum_rows(whole_heads, w_out, False)
    scale_mlp = norm_scale(middle)
    normed_mlp = (middle * scale_mlp[:, None] * gain_mlp).astype(jnp.bfloat16)
    whole_mlp = gather_rows(normed_mlp)
    before = sum_cols(whole_mlp, w_up, False) + b_up
    hidden = jax.nn.silu(before).astype(jnp.bfloat16)
    whole_hidden = gather_cols(hidden)
    result = middle + sum_rows(whole_hidden, w_down, False) + b_down
    saved_state = (
        scale_attn,
        whole_attn,
        raw_queries,
        queries,
        key_rows,
        values,
        log_mass,
        whole_heads,
        middle,
        scale_mlp,
        whole_mlp,
        before,
        whole_hidden,
        factor,
    )
    return (result, saved_state)


def spread_out(vector, length, slot_index):
    return lax.dynamic_update_slice(
        jnp.zeros((length,), jnp.float32), vector, (slot_index * vector.shape[0],)
    )


def take_own(vector, slot_index, slot_width):
    return lax.dynamic_slice(vector, (slot_index * slot_width,), (slot_width,))


def shards(
    tokens,
    prefix,
    gain_attn,
    w_qkv,
    query_scale,
    w_out,
    gain_mlp,
    w_up,
    b_up,
    w_down,
    b_down,
    cotangent,
):
    result, saved_state = forward(
        tokens, prefix, gain_attn, w_qkv, query_scale, w_out, gain_mlp, w_up, b_up, w_down, b_down
    )
    fresh_inputs = lax.optimization_barrier(
        (
            (
                tokens,
                prefix,
                gain_attn,
                w_qkv,
                query_scale,
                w_out,
                gain_mlp,
                w_up,
                b_up,
                w_down,
                b_down,
            ),
            result,
        )
    )[0]
    saved_state = forward(
        fresh_inputs[0],
        fresh_inputs[1],
        fresh_inputs[2],
        fresh_inputs[3],
        fresh_inputs[4],
        fresh_inputs[5],
        fresh_inputs[6],
        fresh_inputs[7],
        fresh_inputs[8],
        fresh_inputs[9],
        fresh_inputs[10],
    )[1]
    (
        scale_attn,
        whole_attn,
        raw_queries,
        queries,
        key_rows,
        values,
        log_mass,
        whole_heads,
        middle,
        scale_mlp,
        whole_mlp,
        before,
        whole_hidden,
        factor,
    ) = saved_state
    head_count = w_qkv.shape[1]
    seq_count = prefix.shape[0]
    grad_out = cotangent.astype(jnp.float32)
    whole_grad = gather_rows(cotangent)
    d_down = contract_rows(whole_hidden, whole_grad)
    d_hidden = sum_cols(whole_grad, w_down, True)
    gate_sig = jax.nn.sigmoid(before)
    d_before = (d_hidden * gate_sig * (1.0 + before * (1.0 - gate_sig))).astype(jnp.bfloat16)
    whole_before = gather_cols(d_before)
    d_up = contract_rows(whole_mlp, whole_before)
    d_normed_mlp = sum_rows(whole_before, w_up, True)
    d_middle_norm, d_gain_mlp = norm_back(d_normed_mlp, middle, scale_mlp, gain_mlp)
    d_middle = grad_out + d_middle_norm
    whole_middle = gather_rows(d_middle.astype(jnp.bfloat16))
    d_out = contract_rows(whole_heads, whole_middle)
    d_attended = (
        sum_cols(whole_middle, w_out, True).astype(jnp.bfloat16).reshape(-1, head_count, HD)
    )
    d_queries, d_keys, d_values = lax.map(
        attend_backward,
        (
            split_sequences(queries, seq_count),
            split_sequences(key_rows, seq_count),
            split_sequences(values, seq_count),
            split_sequences(d_attended, seq_count),
            log_mass,
            prefix,
        ),
    )
    d_queries = d_queries.reshape(-1, head_count, HD)
    d_factor = jnp.sum(d_queries * raw_queries, axis=(0, 1))
    d_query_scale = d_factor * (QK_BASE / math.sqrt(HD)) * jax.nn.sigmoid(query_scale)
    d_mixed = jnp.stack(
        [
            (d_queries * factor).astype(jnp.bfloat16),
            d_keys.reshape(-1, head_count, HD),
            d_values.reshape(-1, head_count, HD),
        ],
        axis=2,
    ).reshape(d_queries.shape[0], -1)
    whole_mixed = gather_cols(d_mixed)
    d_qkv = contract_rows(whole_attn, whole_mixed)
    d_normed_attn = sum_rows(whole_mixed, w_qkv.reshape(w_qkv.shape[0], -1), True)
    d_rows_norm, d_gain_attn = norm_back(
        d_normed_attn, tokens.astype(jnp.float32), scale_attn, gain_attn
    )
    d_tokens = d_middle + d_rows_norm
    col_index = lax.axis_index("col")
    row_index = lax.axis_index("row")
    d_b_up = jnp.sum(d_before.astype(jnp.float32), axis=0)
    d_b_down = jnp.sum(grad_out, axis=0)
    smalls = lax.psum(
        (
            spread_out(d_gain_attn, D, col_index),
            spread_out(d_gain_mlp, D, col_index),
            spread_out(d_b_up, FF, row_index),
            spread_out(d_b_down, D, col_index),
            d_query_scale,
        ),
        ("batch", "row", "col"),
    )
    weights = lax.psum((d_qkv, d_out, d_up, d_down), "batch")
    feature_width = gain_attn.shape[0]
    return (
        result.astype(jnp.bfloat16),
        d_tokens,
        take_own(smalls[0], col_index, feature_width),
        weights[0].reshape(w_qkv.shape),
        smalls[4],
        weights[1],
        take_own(smalls[1], col_index, feature_width),
        weights[2],
        take_own(smalls[2], row_index, b_up.shape[0]),
        weights[3],
        take_own(smalls[3], col_index, feature_width),
    )


def solution(mesh):
    in_specs = (
        P(("batch", "row"), "col"),
        P(("batch", "col")),
        P("col"),
        P("col", "row", None),
        P(),
        P("row", "col"),
        P("col"),
        P("col", "row"),
        P("row"),
        P("row", "col"),
        P("col"),
        P(("batch", "row"), "col"),
    )
    out_specs = (
        P(("batch", "row"), "col"),
        P(("batch", "row"), "col"),
        P("col"),
        P("col", "row", None),
        P(),
        P("row", "col"),
        P("col"),
        P("col", "row"),
        P("row"),
        P("row", "col"),
        P("col"),
    )
    shape = dict(mesh.shape)
    sizes = (shape["batch"], shape["row"], shape["col"])
    gathered = sizes == (4, 2, 4)
    return jax.shard_map(
        gathered_plan(*sizes) if gathered else shards,
        mesh=mesh,
        in_specs=in_specs,
        out_specs=out_specs,
        check_vma=False,
    )
```
